512 devices in a mesh: term: 32 (over z, core), row: 16 (over x, y).
Axes of the slice: x: 4, y: 4, z: 16, core: 2. Of those that a mesh axis runs over, the one named last changes fastest.
Arguments:
- psi: bfloat16 [2048, 2048], P('row'), may hold values from -6 to 6
- left_ops: bfloat16 [32, 2048, 2048], P('term', 'row'), may hold values from -0.0234375 to 0.0234375
- right_ops: bfloat16 [32, 2048, 2048], P('term', 'row'), may hold values from -0.25 to 0.25
- block_mask: int32 [32, 16, 16], P('term', 'row'), may hold values from 0 to 1, as said below
Outputs:
- sigma: bfloat16 [2048, 2048], P('row', 'term')
The draws below stay inside these ranges and needn't reach their ends.
Inputs may be any that keep to these rules, and one draw needn't show every extreme that they name: Entries are 0 or 1; block_mask[t, i, i] = 1 for every term and block.
All inputs are finite; a program needn't handle non-finite values.
Results may differ from the reference program's by a relative error of at most 0.0049.
Values may be sent and summed in bfloat16 or wider, within the bound.
A program may use at most 64 MiB of HBM per device.

```python
import jax
import jax.numpy as jnp
from jax import lax

S = 2048
BLK = 128
NB = 16
TERMS = 32


def draw_block_mask(key, part):
    first, second = jax.random.split(jax.random.fold_in(key, 7))
    level = jax.random.randint(first, (TERMS, 1, 1), 1, 9)
    coins = jax.random.randint(second, (TERMS, NB, NB), 0, 8)
    diagonal = jnp.eye(NB, dtype=jnp.int32)
    return jnp.maximum((coins < level).astype(jnp.int32), diagonal[None])


def raised(drawn, key, source, target, shards_of, factor):
    def block_of(position):
        return (jnp.arange(drawn.shape[position]) // (drawn.shape[position] // shards_of)).reshape((-1,) + (1,) * (drawn.ndim - 1 - position))

    near = jax.random.permutation(key, shards_of)[block_of(target)]
    second = (block_of(target) + shards_of // 2) % shards_of
    return jnp.where((block_of(source) == near) | (block_of(source) == second), factor * drawn, drawn)


def steps_of(key, shape, cuts, least, high):
    factor_of = 1.0
    for axis_at, blocks in cuts:
        heights = jax.random.uniform(jax.random.fold_in(jax.random.fold_in(key, 6), axis_at), (blocks,), jnp.float32, least / len(cuts), high / len(cuts))
        factor_of = factor_of * jnp.repeat(jnp.exp(heights), shape[axis_at] // blocks).reshape((-1,) + (1,) * (len(shape) - 1 - axis_at))
    return factor_of


def bell_draw(key, shape, deviation, bound, cuts=(), kind=jnp.bfloat16):
    entries = deviation * jax.random.normal(key, shape, jnp.float32)
    if cuts:
        entries = entries * steps_of(key, shape, cuts, -0.22, 0.18)
    return jnp.clip(entries, -bound, bound).astype(kind)


def bell_draw_with(rng, shape, width, reach, pieces, heavy, held_as=jnp.bfloat16):
    array = width * jax.random.normal(rng, shape, jnp.float32)
    if pieces:
        array = array * steps_of(rng, shape, pieces, -0.22, 0.18)
    return jnp.clip(raised(array, jax.random.fold_in(rng, 3), *heavy), -reach, reach).astype(held_as)


def setup_inputs(seed: int = 0) -> dict:
    streams_of = jax.random.split(jax.random.key(seed), 5)
    return {
        "psi": bell_draw(streams_of[0], (S, S), 1.0, 6.0, ((0, 16),)),
        "left_ops": bell_draw(streams_of[1], (TERMS, S, S), (S * TERMS) ** -0.5, 0.0234375, ((0, 32), (1, 16))),
        "right_ops": bell_draw_with(streams_of[2], (TERMS, S, S), S ** -0.5, 0.25, ((0, 32), (1, 16)), (0, 1, 32, 2.75)),
        "block_mask": draw_block_mask(jax.random.fold_in(streams_of[4], 71), 0),
    }


def expand_mask(mask):
    blocks = mask.shape[0]
    grid = jnp.broadcast_to(mask[:, None, :, None], (blocks, BLK, blocks, BLK))
    return grid.reshape(blocks * BLK, blocks * BLK)


def reference(psi, left_ops, right_ops, block_mask):
    psi_wide = psi.astype(jnp.float32)

    def one_term(total, items):
        left, right, mask = items
        masked = left * expand_mask(mask).astype(jnp.bfloat16)
        inner = jnp.dot(masked.astype(jnp.float32), psi_wide).astype(jnp.bfloat16)
        total = total + jnp.dot(inner.astype(jnp.float32), right.astype(jnp.float32).T)
        return total, None

    start = jnp.zeros((S, S), jnp.float32)
    total, unused = lax.scan(one_term, start, (left_ops, right_ops, block_mask))
    return total.astype(jnp.bfloat16)
```

```python
import jax
import jax.numpy as jnp
from jax import lax
from jax.experimental import pallas as pl
from jax.experimental.pallas import tpu as pltpu
from jax.sharding import PartitionSpec as P

MESH = pl.DeviceIdType.MESH
N = 4
NZ = 16
B = 128
CH = 32
W = 2048
F32 = jnp.float32
BF16 = jnp.bfloat16


def dot_nt(a, b):
    return lax.dot_general(a, b, (((1,), (1,)), ((), ())), preferred_element_type=F32)


def kernel(
    psi, left, right, mask, out,
    p_buf, r_buf, m_buf, l_buf, q_buf, s_buf, e_buf, t_buf, g_buf,
    load_sem, rs, rr, ps, pr, fs, ms, mr, qs, qr, es, er, zs, zr, hs,
):
    t = lax.axis_index("term")
    row = lax.axis_index("row")
    z, c = t // 2, t % 2
    x, y = row // N, row % N
    xl, xr, xo = (x + 3) % N, (x + 1) % N, (x + 2) % N
    yl, yr, yo = (y + 3) % N, (y + 1) % N, (y + 2) % N
    to_xl, to_xr = (t, xl * N + y), (t, xr * N + y)
    to_yl, to_yr = (t, x * N + yl), (t, x * N + yr)
    twin = (z * 2 + 1 - c, row)

    def along_z(step):
        return (((z + step + NZ) % NZ) * 2 + c, row)

    sent = []

    def send(src, dst, ssem, rsem, device):
        copy = pltpu.make_async_remote_copy(
            src_ref=src, dst_ref=dst, send_sem=ssem, recv_sem=rsem, device_id=device, device_id_type=MESH
        )
        copy.start()
        sent.append(copy)

    def arrived(dst, rsem):
        pltpu.make_async_remote_copy(
            src_ref=dst, dst_ref=dst, send_sem=rsem, recv_sem=rsem, device_id=twin, device_id_type=MESH
        ).wait_recv()

    load_r = pltpu.make_async_copy(right.at[0], r_buf.at[x], load_sem.at[0])
    load_p = pltpu.make_async_copy(psi, p_buf.at[y], load_sem.at[1])
    load_l = pltpu.make_async_copy(left.at[0], l_buf, load_sem.at[2])
    load_l.start()
    load_p.start()
    load_r.start()

    barrier = pltpu.get_barrier_semaphore()
    peers = [to_xl, to_xr, twin, along_z(1), along_z(-1)]
    for other in (yl, yr, yo):
        peers += [(t, x * N + other), (z * 2 + 1 - c, x * N + other)]
    for peer in peers:
        pl.semaphore_signal(barrier, inc=1, device_id=peer, device_id_type=MESH)

    load_l.wait()
    for k in range(W // B):
        scale = jnp.full((B, B), mask[0, 0, k].astype(F32), F32).astype(BF16)
        m_buf[y, :, k * B : (k + 1) * B] = l_buf[:, k * B : (k + 1) * B] * scale

    pl.semaphore_wait(barrier, len(peers))

    def greet(k, distance):
        pl.semaphore_signal(hs.at[k, 0], inc=1, device_id=along_z(distance), device_id_type=MESH)
        if 2 * distance < NZ:
            pl.semaphore_signal(hs.at[k, 1], inc=1, device_id=along_z(-distance), device_id_type=MESH)

    def greeted(k, distance):
        pl.semaphore_wait(hs.at[k, 0], 1)
        if 2 * distance < NZ:
            pl.semaphore_wait(hs.at[k, 1], 1)

    def rows(k):
        return pl.ds(k * CH, CH)

    greet(0, 1)
    lo = 2 * c
    for step in range(4):
        ahead, back = step, (step + 2) % 4
        send(right.at[0, rows(ahead)], r_buf.at[x, rows(ahead)], rs.at[0, step], rr.at[x, ahead], to_xr)
        send(right.at[0, rows(back)], r_buf.at[x, rows(back)], rs.at[1, step], rr.at[x, back], to_xl)
        if step < 2:
            ahead, back = lo + step, lo + 1 - step
            send(psi.at[rows(ahead)], p_buf.at[y, rows(ahead)], ps.at[0, step], pr.at[y, ahead], to_yr)
            send(psi.at[rows(back)], p_buf.at[y, rows(back)], ps.at[1, step], pr.at[y, back], to_yl)
    for step in range(4):
        ahead, back = step, (step + 2) % 4
        send(m_buf.at[y, rows(ahead)], m_buf.at[y, rows(ahead)], ms.at[0, step], mr.at[y, ahead], to_yr)
        send(m_buf.at[y, rows(back)], m_buf.at[y, rows(back)], ms.at[1, step], mr.at[y, back], to_yl)

    def take(buf, sem, block, k):
        arrived(buf.at[block, rows(k)], sem.at[block, k])

    def relay(buf, ssem, sem, block, k, device):
        take(buf, sem, block, k)
        send(buf.at[block, rows(k)], buf.at[block, rows(k)], ssem, sem.at[block, k], device)

    def share(block, k, n):
        send(p_buf.at[block, rows(k)], p_buf.at[block, rows(k)], fs.at[n], pr.at[block, k], twin)

    relay(p_buf, ps.at[0, 2], pr, yl, lo, to_yr)
    share(yl, lo, 0)
    relay(p_buf, ps.at[1, 2], pr, yr, lo + 1, to_yl)
    share(yr, lo + 1, 1)
    relay(r_buf, rs.at[0, 4], rr, xl, 0, to_xr)
    relay(r_buf, rs.at[1, 4], rr, xr, 2, to_xl)
    greeted(0, 1)
    greet(1, 2)
    take(p_buf, pr, yl, lo + 1)
    share(yl, lo + 1, 2)
    take(p_buf, pr, yr, lo)
    share(yr, lo, 3)
    relay(r_buf, rs.at[0, 5], rr, xl, 1, to_xr)
    relay(r_buf, rs.at[1, 5], rr, xr, 3, to_xl)
    greeted(1, 2)
    greet(2, 4)
    take(p_buf, pr, yo, lo)
    share(yo, lo, 4)
    take(p_buf, pr, yo, lo + 1)
    share(yo, lo + 1, 5)
    for block in (yl, yr, yo):
        for k in range(2):
            take(p_buf, pr, block, 2 - lo + k)
    load_p.wait()
    load_r.wait()

    def products(block):
        for half in range(2):
            value = dot_nt(r_buf[block], p_buf[2 * half : 2 * half + 2].reshape(2 * B, W))
            q_buf[block, x, :, 2 * half * B : 2 * (half + 1) * B] = value.astype(BF16)

    products(x)
    greeted(2, 4)
    greet(3, 8)
    take(r_buf, rr, xl, 2)
    take(r_buf, rr, xl, 3)
    products(xl)
    relay(m_buf, ms.at[0, 4], mr, yl, 0, to_yr)
    relay(m_buf, ms.at[1, 4], mr, yr, 2, to_yl)
    take(r_buf, rr, xr, 0)
    take(r_buf, rr, xr, 1)
    products(xr)
    relay(m_buf, ms.at[0, 5], mr, yl, 1, to_yr)
    relay(m_buf, ms.at[1, 5], mr, yr, 3, to_yl)
    for k in (0, 2, 1, 3):
        take(r_buf, rr, xo, k)
    products(xo)

    near = ((y - z) % N + NZ + 1) % N - 1
    first = ((z + near + NZ) % NZ) // N
    order = [(first + k) % N for k in (2, 1, 3, 0)]

    def spread(u):
        ab = order[u]
        send(q_buf.at[ab, x], q_buf.at[ab, x], qs.at[0, u], qr.at[ab, x, 0], to_xr)
        send(q_buf.at[ab, x], q_buf.at[ab, x], qs.at[1, u], qr.at[ab, x, 0], to_xl)

    def pass_on(u):
        ab = order[u]
        arrived(q_buf.at[ab, xl], qr.at[ab, xl, 0])
        part = q_buf.at[ab, xl, pl.ds(0, B // 2)]
        send(part, part, qs.at[2, u], qr.at[ab, xl, 0], to_xr)
        arrived(q_buf.at[ab, xr], qr.at[ab, xr, 0])
        part = q_buf.at[ab, xr, pl.ds(B // 2, B // 2)]
        send(part, part, qs.at[3, u], qr.at[ab, xr, 1], to_xl)

    def last_part(u):
        ab = order[u]
        arrived(q_buf.at[ab, xo, pl.ds(0, B // 2)], qr.at[ab, xo, 0])
        arrived(q_buf.at[ab, xo, pl.ds(B // 2, B // 2)], qr.at[ab, xo, 1])

    def terms(u, blocks, add):
        ab = order[u]
        for half in range(2):
            total = s_buf[u, half] if add else None
            for xk in blocks:
                cols = pl.ds(pl.multiple_of(xk * N * B, N * B), N * B)
                rhs = m_buf[2 * half : 2 * half + 2, :, cols].reshape(2 * B, N * B)
                value = dot_nt(q_buf[ab, xk], rhs)
                total = value if total is None else total + value
            s_buf[u, half] = total

    def exchange(u):
        send(s_buf.at[u, 1 - c], e_buf.at[u], es.at[u], er.at[u], twin)

    homes = []

    def home(u):
        arrived(e_buf.at[u], er.at[u])
        total = (s_buf[u, c] + e_buf[u]).astype(BF16)
        z2 = order[u] * N + y
        for j in range(2):
            t_buf[u, j] = total[:, j * B : (j + 1) * B]
        for c2 in range(2):
            for j in range(2):
                y2 = 2 * c + j
                mine = (z2 == z) & (c == c2) & (y == y2)
                src = t_buf.at[u, j, pl.ds(c2 * B // 2, B // 2)]
                local = pltpu.make_async_copy(src, g_buf.at[z], zr)
                away = pltpu.make_async_remote_copy(
                    src_ref=src, dst_ref=g_buf.at[z], send_sem=zs.at[u, 2 * c2 + j], recv_sem=zr,
                    device_id=(z2 * 2 + c2, x * N + y2), device_id_type=MESH,
                )
                pl.when(mine)(local.start)
                pl.when(jnp.logical_not(mine))(away.start)
                homes.append((mine, away))

    spread(0)
    spread(1)
    for block, ks in ((yl, (2, 3)), (yr, (0, 1))):
        for k in ks:
            take(m_buf, mr, block, k)
    pass_on(0)
    spread(2)
    for k in (0, 2, 1, 3):
        take(m_buf, mr, yo, k)
    pass_on(1)
    spread(3)
    last_part(0)
    terms(0, (0, 1, 2, 3), False)
    exchange(0)
    greeted(3, 8)
    pass_on(2)
    home(0)
    last_part(1)
    terms(1, (0, 1, 2, 3), False)
    exchange(1)
    pass_on(3)
    home(1)
    last_part(2)
    terms(2, (0, 1, 2, 3), False)
    exchange(2)
    terms(3, (x, xl, xr), False)
    home(2)
    last_part(3)
    terms(3, (xo,), True)
    exchange(3)
    home(3)

    pltpu.make_async_copy(g_buf, g_buf, zr).wait()
    total = g_buf[0].astype(F32)
    for k in range(1, NZ):
        total = total + g_buf[k].astype(F32)
    out[...] = jnp.transpose(total).astype(BF16)

    for copy in sent:
        copy.wait_send()
    for mine, away in homes:
        pl.when(jnp.logical_not(mine))(away.wait_send)


def shards(psi, left, right, mask):
    dma = pltpu.SemaphoreType.DMA
    anywhere = pl.BlockSpec(memory_space=pl.ANY)
    return pl.pallas_call(
        kernel,
        out_shape=jax.ShapeDtypeStruct((B, B // 2), BF16),
        in_specs=[anywhere, anywhere, anywhere, pl.BlockSpec(memory_space=pltpu.SMEM)],
        out_specs=pl.BlockSpec(memory_space=pltpu.VMEM),
        scratch_shapes=[
            pltpu.VMEM((N, B, W), BF16),
            pltpu.VMEM((N, B, W), BF16),
            pltpu.VMEM((N, B, W), BF16),
            pltpu.VMEM((B, W), BF16),
            pltpu.VMEM((N, N, B, N * B), BF16),
            pltpu.VMEM((N, 2, B, 2 * B), F32),
            pltpu.VMEM((N, B, 2 * B), F32),
            pltpu.VMEM((N, 2, B, B), BF16),
            pltpu.VMEM((NZ, B // 2, B), BF16),
            dma((3,)),
            dma((2, 6)), dma((N, 4)),
            dma((2, 3)), dma((N, 4)), dma((6,)),
            dma((2, 6)), dma((N, 4)),
            dma((4, N)), dma((N, N, 2)),
            dma((N,)), dma((N,)),
            dma((N, 4)), dma,
            pltpu.SemaphoreType.REGULAR((4, 2)),
        ],
        compiler_params=pltpu.CompilerParams(
            collective_id=0, has_side_effects=True, vmem_limit_bytes=60 << 20
        ),
    )(psi, left, right, mask)


def solution(mesh):
    in_specs = (P("row", None), P("term", "row", None), P("term", "row", None), P("term", "row", None))
    return jax.shard_map(
        shards, mesh=mesh, in_specs=in_specs, out_specs=P("row", "term"), check_vma=False
    )
```

```python
import jax
import jax.numpy as jnp
from jax import lax
from jax.experimental import pallas as pl
from jax.experimental.pallas import tpu as pltpu
from jax.sharding import PartitionSpec as P

MESH = pl.DeviceIdType.MESH
N = 4
NZ = 16
B = 128
CH = 32
W = 2048
ORDER = ((1, 2, 3, 0), (0, 2, 3, 1), (0, 1, 3, 2), (1, 0, 2, 3))
F32 = jnp.float32
BF16 = jnp.bfloat16


def dot_nt(a, b):
    return lax.dot_general(a, b, (((1,), (1,)), ((), ())), preferred_element_type=F32)


def kernel(
    psi, left, right, mask, out,
    p_buf, r_buf, m_buf, l_buf, q_buf, s_buf, e_buf, t_buf, g_buf,
    load_sem, rs, rr, ps, pr, fs, ms, mr, qs, qr, es, er, zs, zr, hs, gs,
):
    t = lax.axis_index("term")
    row = lax.axis_index("row")
    z, c = t // 2, t % 2
    x, y = row // N, row % N
    xl, xr, xo = (x + 3) % N, (x + 1) % N, (x + 2) % N
    yl, yr, yo = (y + 3) % N, (y + 1) % N, (y + 2) % N
    to_xl, to_xr = (t, xl * N + y), (t, xr * N + y)
    to_yl, to_yr = (t, x * N + yl), (t, x * N + yr)
    twin = (z * 2 + 1 - c, row)

    def along_z(step):
        return (((z + step + NZ) % NZ) * 2 + c, row)

    sent = []

    def send(src, dst, ssem, rsem, device):
        copy = pltpu.make_async_remote_copy(
            src_ref=src, dst_ref=dst, send_sem=ssem, recv_sem=rsem, device_id=device, device_id_type=MESH
        )
        copy.start()
        sent.append(copy)

    def arrived(dst, rsem):
        pltpu.make_async_remote_copy(
            src_ref=dst, dst_ref=dst, send_sem=rsem, recv_sem=rsem, device_id=twin, device_id_type=MESH
        ).wait_recv()

    load_r = pltpu.make_async_copy(right.at[0], r_buf.at[x], load_sem.at[0])
    load_p = pltpu.make_async_copy(psi, p_buf.at[y], load_sem.at[1])
    load_l = pltpu.make_async_copy(left.at[0], l_buf, load_sem.at[2])
    load_l.start()
    load_p.start()
    load_r.start()

    barrier = pltpu.get_barrier_semaphore()
    peers = [to_xl, to_xr, to_yl, to_yr, twin, along_z(1), along_z(-1)]
    for peer in peers:
        pl.semaphore_signal(barrier, inc=1, device_id=peer, device_id_type=MESH)

    load_l.wait()
    for k in range(W // B):
        scale = jnp.full((B, B), mask[0, 0, k].astype(F32), F32).astype(BF16)
        m_buf[y, :, k * B : (k + 1) * B] = l_buf[:, k * B : (k + 1) * B] * scale

    pl.semaphore_wait(barrier, len(peers))

    def greet(k, distance):
        pl.semaphore_signal(hs.at[k, 0], inc=1, device_id=along_z(distance), device_id_type=MESH)
        if 2 * distance < NZ:
            pl.semaphore_signal(hs.at[k, 1], inc=1, device_id=along_z(-distance), device_id_type=MESH)

    def greeted(k, distance):
        pl.semaphore_wait(hs.at[k, 0], 1)
        if 2 * distance < NZ:
            pl.semaphore_wait(hs.at[k, 1], 1)

    def rows(k):
        return pl.ds(k * CH, CH)

    lo = 2 * c
    for step in range(4):
        ahead, back = step, (step + 2) % 4
        if step < 2:
            send(psi.at[rows(lo + step)], p_buf.at[y, rows(lo + step)], ps.at[0, step], pr.at[y, lo + step], to_yr)
            other = lo + 1 - step
            send(psi.at[rows(other)], p_buf.at[y, rows(other)], ps.at[1, step], pr.at[y, other], to_yl)
        send(right.at[0, rows(ahead)], r_buf.at[x, rows(ahead)], rs.at[0, step], rr.at[x, ahead], to_xr)
        send(right.at[0, rows(back)], r_buf.at[x, rows(back)], rs.at[1, step], rr.at[x, back], to_xl)
    for k, device in enumerate((to_yl, to_yr)):
        pl.semaphore_signal(gs.at[k], inc=1, device_id=device, device_id_type=MESH)

    def take(buf, sem, block, k):
        arrived(buf.at[block, rows(k)], sem.at[block, k])

    def relay(buf, ssem, sem, block, k, device):
        take(buf, sem, block, k)
        send(buf.at[block, rows(k)], buf.at[block, rows(k)], ssem, sem.at[block, k], device)

    def share(block, k, n):
        send(p_buf.at[block, rows(k)], p_buf.at[block, rows(k)], fs.at[n], pr.at[block, k], twin)

    relay(p_buf, ps.at[0, 2], pr, yl, lo, to_yr)
    relay(p_buf, ps.at[1, 2], pr, yr, lo + 1, to_yl)
    for step in range(4):
        ahead, back = step, (step + 2) % 4
        send(m_buf.at[y, rows(ahead)], m_buf.at[y, rows(ahead)], ms.at[0, step], mr.at[y, ahead], to_yr)
        send(m_buf.at[y, rows(back)], m_buf.at[y, rows(back)], ms.at[1, step], mr.at[y, back], to_yl)
    share(yl, lo, 0)
    share(yr, lo + 1, 1)
    relay(r_buf, rs.at[0, 4], rr, xl, 0, to_xr)
    relay(r_buf, rs.at[1, 4], rr, xr, 2, to_xl)
    pl.semaphore_wait(gs.at[0], 1)
    pl.semaphore_wait(gs.at[1], 1)
    pl.semaphore_signal(gs.at[2], inc=1, device_id=twin, device_id_type=MESH)
    pl.semaphore_wait(gs.at[2], 1)
    greet(0, 1)
    take(p_buf, pr, yl, lo + 1)
    share(yl, lo + 1, 2)
    take(p_buf, pr, yr, lo)
    share(yr, lo, 3)
    relay(r_buf, rs.at[0, 5], rr, xl, 1, to_xr)
    relay(r_buf, rs.at[1, 5], rr, xr, 3, to_xl)
    greeted(0, 1)
    greet(1, 2)
    take(p_buf, pr, yo, lo)
    share(yo, lo, 4)
    take(p_buf, pr, yo, lo + 1)
    share(yo, lo + 1, 5)
    for block in (yl, yr, yo):
        for k in range(2):
            take(p_buf, pr, block, 2 - lo + k)
    load_p.wait()
    load_r.wait()
    greeted(1, 2)
    greet(2, 4)

    def products(block):
        for half in range(2):
            value = dot_nt(r_buf[block], p_buf[2 * half : 2 * half + 2].reshape(2 * B, W))
            q_buf[block, x, :, 2 * half * B : 2 * (half + 1) * B] = value.astype(BF16)

    group = z // N
    order = [sum((group == k).astype(jnp.int32) * ORDER[k][u] for k in range(N)) for u in range(N)]
    swap = (order[0] == xo).astype(jnp.int32)
    sends = [order[0] + swap * (order[1] - order[0]), order[1] + swap * (order[0] - order[1]), order[2], order[3]]

    products(x)
    take(r_buf, rr, xl, 2)
    take(r_buf, rr, xl, 3)
    products(xl)
    take(r_buf, rr, xr, 0)
    take(r_buf, rr, xr, 1)
    products(xr)
    greeted(2, 4)
    greet(3, 8)
    relay(m_buf, ms.at[0, 4], mr, yl, 0, to_yr)
    relay(m_buf, ms.at[1, 4], mr, yr, 2, to_yl)

    def spread(u):
        ab = sends[u]
        send(q_buf.at[ab, x], q_buf.at[ab, x], qs.at[0, u], qr.at[ab, x, 0], to_xr)
        send(q_buf.at[ab, x], q_buf.at[ab, x], qs.at[1, u], qr.at[ab, x, 0], to_xl)

    def pass_on(u):
        ab = order[u]
        arrived(q_buf.at[ab, xl], qr.at[ab, xl, 0])
        part = q_buf.at[ab, xl, pl.ds(0, B // 2)]
        send(part, part, qs.at[2, u], qr.at[ab, xl, 0], to_xr)
        arrived(q_buf.at[ab, xr], qr.at[ab, xr, 0])
        part = q_buf.at[ab, xr, pl.ds(B // 2, B // 2)]
        send(part, part, qs.at[3, u], qr.at[ab, xr, 1], to_xl)

    def last_part(u):
        ab = order[u]
        arrived(q_buf.at[ab, xo, pl.ds(0, B // 2)], qr.at[ab, xo, 0])
        arrived(q_buf.at[ab, xo, pl.ds(B // 2, B // 2)], qr.at[ab, xo, 1])

    def terms(u, blocks, add):
        ab = order[u]
        for half in range(2):
            total = s_buf[u, half] if add else None
            for xk in blocks:
                cols = pl.ds(pl.multiple_of(xk * N * B, N * B), N * B)
                rhs = m_buf[2 * half : 2 * half + 2, :, cols].reshape(2 * B, N * B)
                value = dot_nt(q_buf[ab, xk], rhs)
                total = value if total is None else total + value
            s_buf[u, half] = total

    def exchange(u):
        send(s_buf.at[u, 1 - c], e_buf.at[u], es.at[u], er.at[u], twin)

    homes = []

    def deliver(src, z2, c2, y2, slot, ssem):
        mine = (z2 == z) & (c == c2) & (y == y2)
        local = pltpu.make_async_copy(src, g_buf.at[slot], zr)
        away = pltpu.make_async_remote_copy(
            src_ref=src, dst_ref=g_buf.at[slot], send_sem=ssem, recv_sem=zr,
            device_id=(z2 * 2 + c2, x * N + y2), device_id_type=MESH,
        )
        pl.when(mine)(local.start)
        pl.when(jnp.logical_not(mine))(away.start)
        homes.append((mine, away))

    def home(u):
        arrived(e_buf.at[u], er.at[u])
        total = (s_buf[u, c] + e_buf[u]).astype(BF16)
        for j in range(2):
            t_buf[u, j] = total[:, j * B : (j + 1) * B]
        for c2 in range(2):
            for j in range(2):
                src = t_buf.at[u, j, pl.ds(c2 * B // 2, B // 2)]
                deliver(src, order[u] * N + y, c2, 2 * c + j, z, zs.at[u, 2 * c2 + j])

    def home_apart():
        for y2 in range(N):
            for c2 in range(2):
                src = t_buf.at[3 + y2 // 2, y2 % 2, pl.ds(c2 * B // 2, B // 2)]
                slot = jnp.where(c == y2 // 2, z, NZ + z % N)
                deliver(src, group * N + y, c2, y2, slot, zs.at[3 + y2 // 2, 2 * c2 + y2 % 2])

    spread(0)
    relay(m_buf, ms.at[0, 5], mr, yl, 1, to_yr)
    relay(m_buf, ms.at[1, 5], mr, yr, 3, to_yl)
    for k in (0, 2, 1, 3):
        take(r_buf, rr, xo, k)
    products(xo)
    spread(1)
    for block, ks in ((yl, (2, 3)), (yr, (0, 1))):
        for k in ks:
            take(m_buf, mr, block, k)
    pass_on(0)
    spread(2)
    pass_on(1)
    spread(3)
    for k in (0, 2, 1, 3):
        take(m_buf, mr, yo, k)
    last_part(0)
    terms(0, (0, 1, 2, 3), False)
    exchange(0)
    greeted(3, 8)
    home(0)
    pass_on(2)
    last_part(1)
    terms(1, (0, 1, 2, 3), False)
    exchange(1)
    home(1)
    pass_on(3)
    last_part(2)
    terms(2, (0, 1, 2, 3), False)
    exchange(2)
    terms(3, (x, xl, xr), False)
    home(2)
    last_part(3)
    terms(3, (xo,), True)
    for half in range(2):
        for j in range(2):
            t_buf[3 + half, j] = s_buf[3, half, :, j * B : (j + 1) * B].astype(BF16)
    home_apart()

    pltpu.make_async_copy(g_buf, g_buf, zr).wait()
    total = g_buf[0].astype(F32)
    for k in range(1, NZ + N):
        total = total + g_buf[k].astype(F32)
    out[...] = total.astype(BF16)

    for copy in sent:
        copy.wait_send()
    for mine, away in homes:
        pl.when(jnp.logical_not(mine))(away.wait_send)


def shards(psi, left, right, mask):
    dma = pltpu.SemaphoreType.DMA
    anywhere = pl.BlockSpec(memory_space=pl.ANY)
    return pl.pallas_call(
        kernel,
        out_shape=jax.ShapeDtypeStruct((B // 2, B), BF16),
        in_specs=[anywhere, anywhere, anywhere, pl.BlockSpec(memory_space=pltpu.SMEM)],
        out_specs=pl.BlockSpec(memory_space=pltpu.VMEM),
        scratch_shapes=[
            pltpu.VMEM((N, B, W), BF16),
            pltpu.VMEM((N, B, W), BF16),
            pltpu.VMEM((N, B, W), BF16),
            pltpu.VMEM((B, W), BF16),
            pltpu.VMEM((N, N, B, N * B), BF16),
            pltpu.VMEM((N, 2, B, 2 * B), F32),
            pltpu.VMEM((N - 1, B, 2 * B), F32),
            pltpu.VMEM((N + 1, 2, B, B), BF16),
            pltpu.VMEM((NZ + N, B // 2, B), BF16),
            dma((3,)),
            dma((2, 6)), dma((N, 4)),
            dma((2, 3)), dma((N, 4)), dma((6,)),
            dma((2, 6)), dma((N, 4)),
            dma((4, N)), dma((N, N, 2)),
            dma((N - 1,)), dma((N - 1,)),
            dma((N + 1, 4)), dma,
            pltpu.SemaphoreType.REGULAR((4, 2)), pltpu.SemaphoreType.REGULAR((3,)),
        ],
        compiler_params=pltpu.CompilerParams(
            collective_id=0, has_side_effects=True, vmem_limit_bytes=60 << 20
        ),
    )(psi, left, right, mask).T


def solution(mesh):
    in_specs = (P("row", None), P("term", "row", None), P("term", "row", None), P("term", "row", None))
    return jax.shard_map(
        shards, mesh=mesh, in_specs=in_specs, out_specs=P("row", "term"), check_vma=False
    )
```

```python
import jax
import jax.numpy as jnp
from jax import lax
from jax.experimental import pallas as pl
from jax.experimental.pallas import tpu as pltpu
from jax.sharding import PartitionSpec as P

MESH = pl.DeviceIdType.MESH
N = 4
NZ = 16
G = N - 1 + N
B = 128
CH = 32
W = 2048
ORDER = ((1, 2, 3, 0), (0, 2, 3, 1), (0, 1, 3, 2), (0, 1, 2, 3))
F32 = jnp.float32
BF16 = jnp.bfloat16


def dot_nt(a, b):
    return lax.dot_general(a, b, (((1,), (1,)), ((), ())), preferred_element_type=F32)


def kernel(
    psi, left, right, mask, out,
    p_buf, r_buf, m_buf, l_buf, q_buf, s_buf, e_buf, t_buf, g_buf, l1_buf, f_buf,
    load_sem, rs, rr, ps, pr, fs, ms, mr, qs, qr, es, er, zs, zr, l1s, l1r, hs, gs,
):
    t = lax.axis_index("term")
    row = lax.axis_index("row")
    z, c = t // 2, t % 2
    x, y = row // N, row % N
    xl, xr, xo = (x + 3) % N, (x + 1) % N, (x + 2) % N
    yl, yr, yo = (y + 3) % N, (y + 1) % N, (y + 2) % N
    to_xl, to_xr = (t, xl * N + y), (t, xr * N + y)
    to_yl, to_yr = (t, x * N + yl), (t, x * N + yr)
    twin = (z * 2 + 1 - c, row)

    def along_z(step):
        return (((z + step + NZ) % NZ) * 2 + c, row)

    sent = []

    def send(src, dst, ssem, rsem, device):
        copy = pltpu.make_async_remote_copy(
            src_ref=src, dst_ref=dst, send_sem=ssem, recv_sem=rsem, device_id=device, device_id_type=MESH
        )
        copy.start()
        sent.append(copy)

    def arrived(dst, rsem):
        pltpu.make_async_remote_copy(
            src_ref=dst, dst_ref=dst, send_sem=rsem, recv_sem=rsem, device_id=twin, device_id_type=MESH
        ).wait_recv()

    load_r = pltpu.make_async_copy(right.at[0], r_buf.at[x], load_sem.at[0])
    load_p = pltpu.make_async_copy(psi, p_buf.at[y], load_sem.at[1])
    load_l = pltpu.make_async_copy(left.at[0], l_buf, load_sem.at[2])
    load_l.start()
    load_p.start()
    load_r.start()

    barrier = pltpu.get_barrier_semaphore()
    peers = [to_xl, to_xr, to_yl, to_yr, twin, along_z(1), along_z(-1)]
    for peer in peers:
        pl.semaphore_signal(barrier, inc=1, device_id=peer, device_id_type=MESH)

    load_l.wait()
    for k in range(W // B):
        scale = jnp.full((B, B), mask[0, 0, k].astype(F32), F32).astype(BF16)
        m_buf[y, :, k * B : (k + 1) * B] = l_buf[:, k * B : (k + 1) * B] * scale

    pl.semaphore_wait(barrier, len(peers))

    def greet(k, distance):
        pl.semaphore_signal(hs.at[k, 0], inc=1, device_id=along_z(distance), device_id_type=MESH)
        if 2 * distance < NZ:
            pl.semaphore_signal(hs.at[k, 1], inc=1, device_id=along_z(-distance), device_id_type=MESH)

    def greeted(k, distance):
        pl.semaphore_wait(hs.at[k, 0], 1)
        if 2 * distance < NZ:
            pl.semaphore_wait(hs.at[k, 1], 1)

    def rows(k):
        return pl.ds(k * CH, CH)

    lo = 2 * c
    for step in range(4):
        ahead, back = step, (step + 2) % 4
        if step < 2:
            send(psi.at[rows(lo + step)], p_buf.at[y, rows(lo + step)], ps.at[0, step], pr.at[y, lo + step], to_yr)
            other = lo + 1 - step
            send(psi.at[rows(other)], p_buf.at[y, rows(other)], ps.at[1, step], pr.at[y, other], to_yl)
        send(right.at[0, rows(ahead)], r_buf.at[x, rows(ahead)], rs.at[0, step], rr.at[x, ahead], to_xr)
        send(right.at[0, rows(back)], r_buf.at[x, rows(back)], rs.at[1, step], rr.at[x, back], to_xl)
    for k, device in enumerate((to_yl, to_yr)):
        pl.semaphore_signal(gs.at[k], inc=1, device_id=device, device_id_type=MESH)

    def take(buf, sem, block, k):
        arrived(buf.at[block, rows(k)], sem.at[block, k])

    def relay(buf, ssem, sem, block, k, device):
        take(buf, sem, block, k)
        send(buf.at[block, rows(k)], buf.at[block, rows(k)], ssem, sem.at[block, k], device)

    def share(block, k, n):
        send(p_buf.at[block, rows(k)], p_buf.at[block, rows(k)], fs.at[n], pr.at[block, k], twin)

    relay(p_buf, ps.at[0, 2], pr, yl, lo, to_yr)
    relay(p_buf, ps.at[1, 2], pr, yr, lo + 1, to_yl)
    for step in range(4):
        ahead, back = step, (step + 2) % 4
        send(m_buf.at[y, rows(ahead)], m_buf.at[y, rows(ahead)], ms.at[0, step], mr.at[y, ahead], to_yr)
        send(m_buf.at[y, rows(back)], m_buf.at[y, rows(back)], ms.at[1, step], mr.at[y, back], to_yl)
    share(yl, lo, 0)
    share(yr, lo + 1, 1)
    relay(r_buf, rs.at[0, 4], rr, xl, 0, to_xr)
    relay(r_buf, rs.at[1, 4], rr, xr, 2, to_xl)
    pl.semaphore_wait(gs.at[0], 1)
    pl.semaphore_wait(gs.at[1], 1)
    pl.semaphore_signal(gs.at[2], inc=1, device_id=twin, device_id_type=MESH)
    pl.semaphore_wait(gs.at[2], 1)
    greet(0, 1)
    take(p_buf, pr, yl, lo + 1)
    share(yl, lo + 1, 2)
    take(p_buf, pr, yr, lo)
    share(yr, lo, 3)
    relay(r_buf, rs.at[0, 5], rr, xl, 1, to_xr)
    relay(r_buf, rs.at[1, 5], rr, xr, 3, to_xl)
    greeted(0, 1)
    greet(1, 2)
    take(p_buf, pr, yo, lo)
    share(yo, lo, 4)
    take(p_buf, pr, yo, lo + 1)
    share(yo, lo + 1, 5)
    for block in (yl, yr, yo):
        for k in range(2):
            take(p_buf, pr, block, 2 - lo + k)
    load_p.wait()
    load_r.wait()
    greeted(1, 2)
    greet(2, 4)

    def products(block):
        for half in range(2):
            value = dot_nt(r_buf[block], p_buf[2 * half : 2 * half + 2].reshape(2 * B, W))
            q_buf[block, x, :, 2 * half * B : 2 * (half + 1) * B] = value.astype(BF16)

    group = z // N
    order = [sum((group == k).astype(jnp.int32) * ORDER[k][u] for k in range(N)) for u in range(N)]
    swap = (order[0] == xo).astype(jnp.int32)
    sends = [order[0] + swap * (order[1] - order[0]), order[1] + swap * (order[0] - order[1]), order[2], order[3]]

    products(x)
    take(r_buf, rr, xl, 2)
    take(r_buf, rr, xl, 3)
    products(xl)
    take(r_buf, rr, xr, 0)
    take(r_buf, rr, xr, 1)
    products(xr)
    greeted(2, 4)
    greet(3, 8)
    relay(m_buf, ms.at[0, 4], mr, yl, 0, to_yr)
    relay(m_buf, ms.at[1, 4], mr, yr, 2, to_yl)

    def spread(u):
        ab = sends[u]
        send(q_buf.at[ab, x], q_buf.at[ab, x], qs.at[0, u], qr.at[ab, x, 0], to_xr)
        send(q_buf.at[ab, x], q_buf.at[ab, x], qs.at[1, u], qr.at[ab, x, 0], to_xl)

    def pass_on(u):
        ab = order[u]
        arrived(q_buf.at[ab, xl], qr.at[ab, xl, 0])
        part = q_buf.at[ab, xl, pl.ds(0, B // 2)]
        send(part, part, qs.at[2, u], qr.at[ab, xl, 0], to_xr)
        arrived(q_buf.at[ab, xr], qr.at[ab, xr, 0])
        part = q_buf.at[ab, xr, pl.ds(B // 2, B // 2)]
        send(part, part, qs.at[3, u], qr.at[ab, xr, 1], to_xl)

    def last_part(u):
        ab = order[u]
        arrived(q_buf.at[ab, xo, pl.ds(0, B // 2)], qr.at[ab, xo, 0])
        arrived(q_buf.at[ab, xo, pl.ds(B // 2, B // 2)], qr.at[ab, xo, 1])

    def terms(u, blocks, add):
        ab = order[u]
        for half in range(2):
            total = s_buf[u, half] if add else None
            for xk in blocks:
                cols = pl.ds(pl.multiple_of(xk * N * B, N * B), N * B)
                rhs = m_buf[2 * half : 2 * half + 2, :, cols].reshape(2 * B, N * B)
                value = dot_nt(q_buf[ab, xk], rhs)
                total = value if total is None else total + value
            s_buf[u, half] = total

    def exchange(u):
        send(s_buf.at[u, 1 - c], e_buf.at[u], es.at[u], er.at[u], twin)

    homes = []
    place = z % N
    collector = c == place // 2

    def deliver(src, z2, c2, y2, slot, ssem):
        mine = (z2 == z) & (c == c2) & (y == y2)
        local = pltpu.make_async_copy(src, g_buf.at[slot], zr)
        away = pltpu.make_async_remote_copy(
            src_ref=src, dst_ref=g_buf.at[slot], send_sem=ssem, recv_sem=zr,
            device_id=(z2 * 2 + c2, x * N + y2), device_id_type=MESH,
        )
        pl.when(mine)(local.start)
        pl.when(jnp.logical_not(mine))(away.start)
        homes.append((jnp.logical_not(mine), away))

    def gather(u):
        arrived(e_buf.at[u], er.at[u])
        s_buf[u, c] = s_buf[u, c] + e_buf[u]
        for k in range(2):
            t_buf[u, k] = s_buf[u, c, :, k * B : (k + 1) * B].astype(BF16)
            there = 2 * c + k
            away = pltpu.make_async_remote_copy(
                src_ref=t_buf.at[u, k], dst_ref=l1_buf.at[u, place], send_sem=l1s.at[u, k], recv_sem=l1r.at[u, place],
                device_id=((group * N + there) * 2 + c, row), device_id_type=MESH,
            )
            other = there != place
            pl.when(other)(away.start)
            homes.append((other, away))

    def collect(u):
        @pl.when(collector)
        def _():
            total = s_buf[u, c, :, pl.ds(pl.multiple_of((place % 2) * B, B), B)]
            for k in range(1, N):
                source = (place + k) % N
                arrived(l1_buf.at[u, source], l1r.at[u, source])
                total = total + l1_buf[u, source].astype(F32)
            f_buf[u] = total.astype(BF16)
            slot = (group - order[u] + N) % N - 1
            for c2 in range(2):
                pltpu.make_async_remote_copy(
                    src_ref=f_buf.at[u, pl.ds(c2 * B // 2, B // 2)], dst_ref=g_buf.at[slot],
                    send_sem=zs.at[u, c2], recv_sem=zr,
                    device_id=((order[u] * N + y) * 2 + c2, x * N + place), device_id_type=MESH,
                ).start()

    def collected(u):
        @pl.when(collector)
        def _():
            for c2 in range(2):
                pltpu.make_async_remote_copy(
                    src_ref=f_buf.at[u, pl.ds(c2 * B // 2, B // 2)], dst_ref=g_buf.at[0],
                    send_sem=zs.at[u, c2], recv_sem=zr, device_id=twin, device_id_type=MESH,
                ).wait_send()

    def home_own():
        arrived(e_buf.at[3], er.at[3])
        total = (s_buf[3, c] + e_buf[3]).astype(BF16)
        for k in range(2):
            t_buf[3, k] = total[:, k * B : (k + 1) * B]
        for k in range(2):
            for c2 in range(2):
                src = t_buf.at[3, k, pl.ds(c2 * B // 2, B // 2)]
                deliver(src, group * N + y, c2, 2 * c + k, 3 + place, zs.at[3, 2 * c2 + k])

    spread(0)
    relay(m_buf, ms.at[0, 5], mr, yl, 1, to_yr)
    relay(m_buf, ms.at[1, 5], mr, yr, 3, to_yl)
    for k in (0, 2, 1, 3):
        take(r_buf, rr, xo, k)
    products(xo)
    spread(1)
    for block, ks in ((yl, (2, 3)), (yr, (0, 1))):
        for k in ks:
            take(m_buf, mr, block, k)
    pass_on(0)
    spread(2)
    pass_on(1)
    spread(3)
    for k in (0, 2, 1, 3):
        take(m_buf, mr, yo, k)
    last_part(0)
    terms(0, (0, 1, 2, 3), False)
    exchange(0)
    greeted(3, 8)
    gather(0)
    pass_on(2)
    last_part(1)
    terms(1, (0, 1, 2, 3), False)
    exchange(1)
    collect(0)
    gather(1)
    pass_on(3)
    last_part(2)
    terms(2, (0, 1, 2, 3), False)
    exchange(2)
    terms(3, (x, xl, xr), False)
    gather(2)
    collect(1)
    last_part(3)
    terms(3, (xo,), True)
    exchange(3)
    collect(2)
    home_own()

    pltpu.make_async_copy(g_buf, g_buf, zr).wait()
    total = g_buf[0].astype(F32)
    for k in range(1, G):
        total = total + g_buf[k].astype(F32)
    out[...] = total.astype(BF16)

    for copy in sent:
        copy.wait_send()
    for started, away in homes:
        pl.when(started)(away.wait_send)
    for u in range(N - 1):
        collected(u)


def shards(psi, left, right, mask):
    dma = pltpu.SemaphoreType.DMA
    anywhere = pl.BlockSpec(memory_space=pl.ANY)
    return pl.pallas_call(
        kernel,
        out_shape=jax.ShapeDtypeStruct((B // 2, B), BF16),
        in_specs=[anywhere, anywhere, anywhere, pl.BlockSpec(memory_space=pltpu.SMEM)],
        out_specs=pl.BlockSpec(memory_space=pltpu.VMEM),
        scratch_shapes=[
            pltpu.VMEM((N, B, W), BF16),
            pltpu.VMEM((N, B, W), BF16),
            pltpu.VMEM((N, B, W), BF16),
            pltpu.VMEM((B, W), BF16),
            pltpu.VMEM((N, N, B, N * B), BF16),
            pltpu.VMEM((N, 2, B, 2 * B), F32),
            pltpu.VMEM((N, B, 2 * B), F32),
            pltpu.VMEM((N, 2, B, B), BF16),
            pltpu.VMEM((G, B // 2, B), BF16),
            pltpu.VMEM((N - 1, N, B, B), BF16),
            pltpu.VMEM((N - 1, B, B), BF16),
            dma((3,)),
            dma((2, 6)), dma((N, 4)),
            dma((2, 3)), dma((N, 4)), dma((6,)),
            dma((2, 6)), dma((N, 4)),
            dma((4, N)), dma((N, N, 2)),
            dma((N,)), dma((N,)),
            dma((N, 4)), dma, dma((N - 1, 2)), dma((N - 1, N)),
            pltpu.SemaphoreType.REGULAR((4, 2)), pltpu.SemaphoreType.REGULAR((3,)),
        ],
        compiler_params=pltpu.CompilerParams(
            collective_id=0, has_side_effects=True, vmem_limit_bytes=60 << 20
        ),
    )(psi, left, right, mask).T


def solution(mesh):
    in_specs = (P("row", None), P("term", "row", None), P("term", "row", None), P("term", "row", None))
    return jax.shard_map(
        shards, mesh=mesh, in_specs=in_specs, out_specs=P("row", "term"), check_vma=False
    )
```

```python
import jax
import jax.numpy as jnp
from jax import lax
from jax.experimental import pallas as pl
from jax.experimental.pallas import tpu as pltpu
from jax.sharding import PartitionSpec as P

MESH = pl.DeviceIdType.MESH
N = 4
NZ = 16
G = N - 1 + N
B = 128
CH = 32
W = 2048
ORDER = ((0, 1, 2, 3), (0, 2, 3, 1), (0, 1, 3, 2), (0, 1, 2, 3))
F32 = jnp.float32
BF16 = jnp.bfloat16


def dot_nt(a, b):
    return lax.dot_general(a, b, (((1,), (1,)), ((), ())), preferred_element_type=F32)


def kernel(
    psi, left, right, mask, out,
    p_buf, r_buf, m_buf, l_buf, q_buf, s_buf, e_buf, t_buf, g_buf, l1_buf, f_buf,
    load_sem, rs, rr, ps, pr, fs, ms, mr, qs, qr, es, er, zs, zr, fz, l1s, l1r, hs, gs,
):
    t = lax.axis_index("term")
    row = lax.axis_index("row")
    z, c = t // 2, t % 2
    x, y = row // N, row % N
    xl, xr, xo = (x + 3) % N, (x + 1) % N, (x + 2) % N
    yl, yr, yo = (y + 3) % N, (y + 1) % N, (y + 2) % N
    to_xl, to_xr = (t, xl * N + y), (t, xr * N + y)
    to_yl, to_yr = (t, x * N + yl), (t, x * N + yr)
    twin = (z * 2 + 1 - c, row)

    def along_z(step):
        return (((z + step + NZ) % NZ) * 2 + c, row)

    sent = []

    def send(src, dst, ssem, rsem, device):
        copy = pltpu.make_async_remote_copy(
            src_ref=src, dst_ref=dst, send_sem=ssem, recv_sem=rsem, device_id=device, device_id_type=MESH
        )
        copy.start()
        sent.append(copy)

    def arrived(dst, rsem):
        pltpu.make_async_remote_copy(
            src_ref=dst, dst_ref=dst, send_sem=rsem, recv_sem=rsem, device_id=twin, device_id_type=MESH
        ).wait_recv()

    load_r = pltpu.make_async_copy(right.at[0], r_buf.at[x], load_sem.at[0])
    load_p = pltpu.make_async_copy(psi, p_buf.at[y], load_sem.at[1])
    load_l = pltpu.make_async_copy(left.at[0], l_buf, load_sem.at[2])
    load_l.start()
    load_p.start()
    load_r.start()

    barrier = pltpu.get_barrier_semaphore()
    peers = [to_xl, to_xr, to_yl, to_yr, twin, along_z(1), along_z(-1)]
    for peer in peers:
        pl.semaphore_signal(barrier, inc=1, device_id=peer, device_id_type=MESH)

    load_l.wait()
    for k in range(W // B):
        scale = jnp.full((B, B), mask[0, 0, k].astype(F32), F32).astype(BF16)
        m_buf[y, :, k * B : (k + 1) * B] = l_buf[:, k * B : (k + 1) * B] * scale

    pl.semaphore_wait(barrier, len(peers))

    def greet(k, distance):
        pl.semaphore_signal(hs.at[k, 0], inc=1, device_id=along_z(distance), device_id_type=MESH)
        if 2 * distance < NZ:
            pl.semaphore_signal(hs.at[k, 1], inc=1, device_id=along_z(-distance), device_id_type=MESH)

    def greeted(k, distance):
        pl.semaphore_wait(hs.at[k, 0], 1)
        if 2 * distance < NZ:
            pl.semaphore_wait(hs.at[k, 1], 1)

    def rows(k):
        return pl.ds(k * CH, CH)

    lo = 2 * c
    for step in range(4):
        ahead, back = step, (step + 2) % 4
        if step < 2:
            send(psi.at[rows(lo + step)], p_buf.at[y, rows(lo + step)], ps.at[0, step], pr.at[y, lo + step], to_yr)
            other = lo + 1 - step
            send(psi.at[rows(other)], p_buf.at[y, rows(other)], ps.at[1, step], pr.at[y, other], to_yl)
        send(right.at[0, rows(ahead)], r_buf.at[x, rows(ahead)], rs.at[0, step], rr.at[x, ahead], to_xr)
        send(right.at[0, rows(back)], r_buf.at[x, rows(back)], rs.at[1, step], rr.at[x, back], to_xl)
    for k, device in enumerate((to_yl, to_yr)):
        pl.semaphore_signal(gs.at[k], inc=1, device_id=device, device_id_type=MESH)

    def take(buf, sem, block, k):
        arrived(buf.at[block, rows(k)], sem.at[block, k])

    def relay(buf, ssem, sem, block, k, device):
        take(buf, sem, block, k)
        send(buf.at[block, rows(k)], buf.at[block, rows(k)], ssem, sem.at[block, k], device)

    def share(block, k, n):
        send(p_buf.at[block, rows(k)], p_buf.at[block, rows(k)], fs.at[n], pr.at[block, k], twin)

    relay(p_buf, ps.at[0, 2], pr, yl, lo, to_yr)
    relay(p_buf, ps.at[1, 2], pr, yr, lo + 1, to_yl)
    for step in range(4):
        ahead, back = step, (step + 2) % 4
        send(m_buf.at[y, rows(ahead)], m_buf.at[y, rows(ahead)], ms.at[0, step], mr.at[y, ahead], to_yr)
        send(m_buf.at[y, rows(back)], m_buf.at[y, rows(back)], ms.at[1, step], mr.at[y, back], to_yl)
    share(yl, lo, 0)
    share(yr, lo + 1, 1)
    relay(r_buf, rs.at[0, 4], rr, xl, 0, to_xr)
    relay(r_buf, rs.at[1, 4], rr, xr, 2, to_xl)
    pl.semaphore_wait(gs.at[0], 1)
    pl.semaphore_wait(gs.at[1], 1)
    pl.semaphore_signal(gs.at[2], inc=1, device_id=twin, device_id_type=MESH)
    pl.semaphore_wait(gs.at[2], 1)
    take(p_buf, pr, yl, lo + 1)
    share(yl, lo + 1, 2)
    take(p_buf, pr, yr, lo)
    share(yr, lo, 3)
    relay(r_buf, rs.at[0, 5], rr, xl, 1, to_xr)
    relay(r_buf, rs.at[1, 5], rr, xr, 3, to_xl)
    greet(0, 1)
    take(p_buf, pr, yo, lo)
    share(yo, lo, 4)
    take(p_buf, pr, yo, lo + 1)
    share(yo, lo + 1, 5)
    for block in (yl, yr, yo):
        for k in range(2):
            take(p_buf, pr, block, 2 - lo + k)
    load_p.wait()
    load_r.wait()
    greeted(0, 1)
    greet(1, 2)

    def products(block):
        for half in range(2):
            value = dot_nt(r_buf[block], p_buf[2 * half : 2 * half + 2].reshape(2 * B, W))
            q_buf[block, x, :, 2 * half * B : 2 * (half + 1) * B] = value.astype(BF16)

    group = z // N
    order = [sum((group == k).astype(jnp.int32) * ORDER[k][u] for k in range(N)) for u in range(N)]
    swap = (order[0] == xo).astype(jnp.int32)
    sends = [order[0] + swap * (order[1] - order[0]), order[1] + swap * (order[0] - order[1]), order[2], order[3]]

    products(x)
    take(r_buf, rr, xl, 2)
    take(r_buf, rr, xl, 3)
    products(xl)
    take(r_buf, rr, xr, 0)
    take(r_buf, rr, xr, 1)
    products(xr)
    greeted(1, 2)
    greet(2, 4)
    relay(m_buf, ms.at[0, 4], mr, yl, 0, to_yr)
    relay(m_buf, ms.at[1, 4], mr, yr, 2, to_yl)

    def spread(u):
        ab = sends[u]
        send(q_buf.at[ab, x], q_buf.at[ab, x], qs.at[0, u], qr.at[ab, x, 0], to_xr)
        send(q_buf.at[ab, x], q_buf.at[ab, x], qs.at[1, u], qr.at[ab, x, 0], to_xl)

    def pass_on(u):
        ab = order[u]
        arrived(q_buf.at[ab, xl], qr.at[ab, xl, 0])
        part = q_buf.at[ab, xl, pl.ds(0, B // 2)]
        send(part, part, qs.at[2, u], qr.at[ab, xl, 0], to_xr)
        arrived(q_buf.at[ab, xr], qr.at[ab, xr, 0])
        part = q_buf.at[ab, xr, pl.ds(B // 2, B // 2)]
        send(part, part, qs.at[3, u], qr.at[ab, xr, 1], to_xl)

    def last_part(u):
        ab = order[u]
        arrived(q_buf.at[ab, xo, pl.ds(0, B // 2)], qr.at[ab, xo, 0])
        arrived(q_buf.at[ab, xo, pl.ds(B // 2, B // 2)], qr.at[ab, xo, 1])

    def terms(u, blocks, add):
        ab = order[u]
        for half in range(2):
            total = s_buf[u, half] if add else None
            for xk in blocks:
                cols = pl.ds(pl.multiple_of(xk * N * B, N * B), N * B)
                rhs = m_buf[2 * half : 2 * half + 2, :, cols].reshape(2 * B, N * B)
                value = dot_nt(q_buf[ab, xk], rhs)
                total = value if total is None else total + value
            s_buf[u, half] = total

    def exchange(u):
        send(s_buf.at[u, 1 - c], e_buf.at[u], es.at[u], er.at[u], twin)

    homes = []
    place = z % N
    collector = c == place // 2

    own = [ab == group for ab in order]

    def start_if(condition, copy):
        pl.when(condition)(copy.start)
        homes.append((condition, copy))

    def gather(u):
        arrived(e_buf.at[u], er.at[u])
        s_buf[u, c] = s_buf[u, c] + e_buf[u]
        for k in range(2):
            t_buf[u, k] = s_buf[u, c, :, k * B : (k + 1) * B].astype(BF16)
            there = 2 * c + k
            away = pltpu.make_async_remote_copy(
                src_ref=t_buf.at[u, k], dst_ref=l1_buf.at[u, place], send_sem=l1s.at[u, k], recv_sem=l1r.at[u, place],
                device_id=((group * N + there) * 2 + c, row), device_id_type=MESH,
            )
            start_if(jnp.logical_not(own[u]) & (there != place), away)
        for k in range(2):
            for c2 in range(2):
                src = t_buf.at[u, k, pl.ds(c2 * B // 2, B // 2)]
                z2, y2, dst = group * N + y, 2 * c + k, g_buf.at[3 + place]
                mine = (z2 == z) & (c == c2) & (y == y2)
                local = pltpu.make_async_copy(src, dst, zr)
                away = pltpu.make_async_remote_copy(
                    src_ref=src, dst_ref=dst, send_sem=zs.at[u, 2 * c2 + k], recv_sem=zr,
                    device_id=(z2 * 2 + c2, x * N + y2), device_id_type=MESH,
                )
                pl.when(own[u] & mine)(local.start)
                start_if(own[u] & jnp.logical_not(mine), away)

    def from_group(u):
        return collector & jnp.logical_not(own[u])

    def collect(u):
        @pl.when(from_group(u))
        def _():
            total = s_buf[u, c, :, pl.ds(pl.multiple_of((place % 2) * B, B), B)]
            for k in range(1, N):
                source = (place + k) % N
                arrived(l1_buf.at[u, source], l1r.at[u, source])
                total = total + l1_buf[u, source].astype(F32)
            f_buf[u] = total.astype(BF16)
            slot = (group - order[u] + N) % N - 1
            for c2 in range(2):
                pltpu.make_async_remote_copy(
                    src_ref=f_buf.at[u, pl.ds(c2 * B // 2, B // 2)], dst_ref=g_buf.at[slot],
                    send_sem=fz.at[u, c2], recv_sem=zr,
                    device_id=((order[u] * N + y) * 2 + c2, x * N + place), device_id_type=MESH,
                ).start()

    def collected(u):
        @pl.when(from_group(u))
        def _():
            for c2 in range(2):
                pltpu.make_async_remote_copy(
                    src_ref=f_buf.at[u, pl.ds(c2 * B // 2, B // 2)], dst_ref=g_buf.at[0],
                    send_sem=fz.at[u, c2], recv_sem=zr, device_id=twin, device_id_type=MESH,
                ).wait_send()

    spread(0)
    relay(m_buf, ms.at[0, 5], mr, yl, 1, to_yr)
    relay(m_buf, ms.at[1, 5], mr, yr, 3, to_yl)
    for k in (0, 2, 1, 3):
        take(r_buf, rr, xo, k)
    products(xo)
    spread(1)
    greeted(2, 4)
    greet(3, 8)
    for block, ks in ((yl, (2, 3)), (yr, (0, 1))):
        for k in ks:
            take(m_buf, mr, block, k)
    pass_on(0)
    spread(2)
    pass_on(1)
    spread(3)
    for k in (0, 2, 1, 3):
        take(m_buf, mr, yo, k)
    last_part(0)
    terms(0, (0, 1, 2, 3), False)
    exchange(0)
    pass_on(2)
    greeted(3, 8)
    gather(0)
    last_part(1)
    terms(1, (0, 1, 2, 3), False)
    exchange(1)
    gather(1)
    pass_on(3)
    collect(0)
    last_part(2)
    terms(2, (0, 1, 2, 3), False)
    exchange(2)
    terms(3, (x, xl, xr), False)
    gather(2)
    collect(1)
    last_part(3)
    terms(3, (xo,), True)
    exchange(3)
    collect(2)
    gather(3)
    collect(3)

    pltpu.make_async_copy(g_buf, g_buf, zr).wait()
    total = g_buf[0].astype(F32)
    for k in range(1, G):
        total = total + g_buf[k].astype(F32)
    out[...] = total.astype(BF16)

    for copy in sent:
        copy.wait_send()
    for started, away in homes:
        pl.when(started)(away.wait_send)
    for u in range(N):
        collected(u)


def shards(psi, left, right, mask):
    dma = pltpu.SemaphoreType.DMA
    anywhere = pl.BlockSpec(memory_space=pl.ANY)
    return pl.pallas_call(
        kernel,
        out_shape=jax.ShapeDtypeStruct((B // 2, B), BF16),
        in_specs=[anywhere, anywhere, anywhere, pl.BlockSpec(memory_space=pltpu.SMEM)],
        out_specs=pl.BlockSpec(memory_space=pltpu.VMEM),
        scratch_shapes=[
            pltpu.VMEM((N, B, W), BF16),
            pltpu.VMEM((N, B, W), BF16),
            pltpu.VMEM((N, B, W), BF16),
            pltpu.VMEM((B, W), BF16),
            pltpu.VMEM((N, N, B, N * B), BF16),
            pltpu.VMEM((N, 2, B, 2 * B), F32),
            pltpu.VMEM((N, B, 2 * B), F32),
            pltpu.VMEM((N, 2, B, B), BF16),
            pltpu.VMEM((G, B // 2, B), BF16),
            pltpu.VMEM((N, N, B, B), BF16),
            pltpu.VMEM((N, B, B), BF16),
            dma((3,)),
            dma((2, 6)), dma((N, 4)),
            dma((2, 3)), dma((N, 4)), dma((6,)),
            dma((2, 6)), dma((N, 4)),
            dma((4, N)), dma((N, N, 2)),
            dma((N,)), dma((N,)),
            dma((N, 4)), dma, dma((N, 2)), dma((N, 2)), dma((N, N)),
            pltpu.SemaphoreType.REGULAR((4, 2)), pltpu.SemaphoreType.REGULAR((3,)),
        ],
        compiler_params=pltpu.CompilerParams(
            collective_id=0, has_side_effects=True, vmem_limit_bytes=60 << 20
        ),
    )(psi, left, right, mask).T


def solution(mesh):
    in_specs = (P("row", None), P("term", "row", None), P("term", "row", None), P("term", "row", None))
    return jax.shard_map(
        shards, mesh=mesh, in_specs=in_specs, out_specs=P("row", "term"), check_vma=False
    )
```

```python
import jax
import jax.numpy as jnp
from jax import lax
from jax.experimental import pallas as pl
from jax.experimental.pallas import tpu as pltpu
from jax.sharding import PartitionSpec as P

MESH = pl.DeviceIdType.MESH
N = 4
NZ = 16
G = N - 1 + N
B = 128
CH = 32
W = 2048
ORDER = ((0, 1, 2, 3), (0, 2, 3, 1), (0, 1, 3, 2), (0, 1, 2, 3))
F32 = jnp.float32
BF16 = jnp.bfloat16


def dot_nt(a, b):
    return lax.dot_general(a, b, (((1,), (1,)), ((), ())), preferred_element_type=F32)


def kernel(
    psi, left, right, mask, out,
    p_buf, r_buf, m_buf, l_buf, q_buf, s_buf, e_buf, t_buf, g_buf, l1_buf, f_buf,
    load_sem, rs, rr, ps, pr, fs, ms, mr, qs, qr, es, er, zs, zr, fz, l1s, l1r, hs, gs,
):
    t = lax.axis_index("term")
    row = lax.axis_index("row")
    z, c = t // 2, t % 2
    x, y = row // N, row % N
    xl, xr, xo = (x + 3) % N, (x + 1) % N, (x + 2) % N
    yl, yr, yo = (y + 3) % N, (y + 1) % N, (y + 2) % N
    to_xl, to_xr = (t, xl * N + y), (t, xr * N + y)
    to_yl, to_yr = (t, x * N + yl), (t, x * N + yr)
    twin = (z * 2 + 1 - c, row)

    def along_z(step):
        return (((z + step + NZ) % NZ) * 2 + c, row)

    sent = []

    def send(src, dst, ssem, rsem, device):
        copy = pltpu.make_async_remote_copy(
            src_ref=src, dst_ref=dst, send_sem=ssem, recv_sem=rsem, device_id=device, device_id_type=MESH
        )
        copy.start()
        sent.append(copy)

    def arrived(dst, rsem):
        pltpu.make_async_remote_copy(
            src_ref=dst, dst_ref=dst, send_sem=rsem, recv_sem=rsem, device_id=twin, device_id_type=MESH
        ).wait_recv()

    load_r = pltpu.make_async_copy(right.at[0], r_buf.at[x], load_sem.at[0])
    load_p = pltpu.make_async_copy(psi, p_buf.at[y], load_sem.at[1])
    load_l = pltpu.make_async_copy(left.at[0], l_buf, load_sem.at[2])
    barrier = pltpu.get_barrier_semaphore()
    peers = [to_xl, to_xr, to_yl, to_yr, twin, along_z(1), along_z(-1)]
    for peer in peers:
        pl.semaphore_signal(barrier, inc=1, device_id=peer, device_id_type=MESH)

    load_l.start()
    load_p.start()
    load_r.start()
    pl.semaphore_wait(barrier, len(peers))

    def greet(k, distance):
        pl.semaphore_signal(hs.at[k, 0], inc=1, device_id=along_z(distance), device_id_type=MESH)
        if 2 * distance < NZ:
            pl.semaphore_signal(hs.at[k, 1], inc=1, device_id=along_z(-distance), device_id_type=MESH)

    def greeted(k, distance):
        pl.semaphore_wait(hs.at[k, 0], 1)
        if 2 * distance < NZ:
            pl.semaphore_wait(hs.at[k, 1], 1)

    def rows(k):
        return pl.ds(k * CH, CH)

    lo = 2 * c
    for step in range(4):
        ahead, back = step, (step + 2) % 4
        if step < 2:
            send(psi.at[rows(lo + step)], p_buf.at[y, rows(lo + step)], ps.at[0, step], pr.at[y, lo + step], to_yr)
            other = lo + 1 - step
            send(psi.at[rows(other)], p_buf.at[y, rows(other)], ps.at[1, step], pr.at[y, other], to_yl)
        send(right.at[0, rows(ahead)], r_buf.at[x, rows(ahead)], rs.at[0, step], rr.at[x, ahead], to_xr)
        send(right.at[0, rows(back)], r_buf.at[x, rows(back)], rs.at[1, step], rr.at[x, back], to_xl)
    for k, device in enumerate((to_yl, to_yr)):
        pl.semaphore_signal(gs.at[k], inc=1, device_id=device, device_id_type=MESH)

    def take(buf, sem, block, k):
        arrived(buf.at[block, rows(k)], sem.at[block, k])

    def relay(buf, ssem, sem, block, k, device):
        take(buf, sem, block, k)
        send(buf.at[block, rows(k)], buf.at[block, rows(k)], ssem, sem.at[block, k], device)

    def share(block, k, n):
        send(p_buf.at[block, rows(k)], p_buf.at[block, rows(k)], fs.at[n], pr.at[block, k], twin)

    load_l.wait()
    for k in range(W // B):
        scale = jnp.full((B, B), mask[0, 0, k].astype(F32), F32).astype(BF16)
        m_buf[y, :, k * B : (k + 1) * B] = l_buf[:, k * B : (k + 1) * B] * scale

    relay(p_buf, ps.at[0, 2], pr, yl, lo, to_yr)
    relay(p_buf, ps.at[1, 2], pr, yr, lo + 1, to_yl)
    for step in range(4):
        ahead, back = step, (step + 2) % 4
        send(m_buf.at[y, rows(ahead)], m_buf.at[y, rows(ahead)], ms.at[0, step], mr.at[y, ahead], to_yr)
        send(m_buf.at[y, rows(back)], m_buf.at[y, rows(back)], ms.at[1, step], mr.at[y, back], to_yl)
    share(yl, lo, 0)
    share(yr, lo + 1, 1)
    relay(r_buf, rs.at[0, 4], rr, xl, 0, to_xr)
    relay(r_buf, rs.at[1, 4], rr, xr, 2, to_xl)
    pl.semaphore_wait(gs.at[0], 1)
    pl.semaphore_wait(gs.at[1], 1)
    pl.semaphore_signal(gs.at[2], inc=1, device_id=twin, device_id_type=MESH)
    pl.semaphore_wait(gs.at[2], 1)
    take(p_buf, pr, yl, lo + 1)
    share(yl, lo + 1, 2)
    take(p_buf, pr, yr, lo)
    share(yr, lo, 3)
    relay(r_buf, rs.at[0, 5], rr, xl, 1, to_xr)
    relay(r_buf, rs.at[1, 5], rr, xr, 3, to_xl)
    greet(0, 1)
    take(p_buf, pr, yo, lo)
    share(yo, lo, 4)
    take(p_buf, pr, yo, lo + 1)
    share(yo, lo + 1, 5)
    for block in (yl, yr, yo):
        for k in range(2):
            take(p_buf, pr, block, 2 - lo + k)
    load_p.wait()
    load_r.wait()
    greeted(0, 1)
    greet(1, 2)

    def products(block):
        for half in range(2):
            value = dot_nt(r_buf[block], p_buf[2 * half : 2 * half + 2].reshape(2 * B, W))
            q_buf[block, x, :, 2 * half * B : 2 * (half + 1) * B] = value.astype(BF16)

    group = z // N
    order = [sum((group == k).astype(jnp.int32) * ORDER[k][u] for k in range(N)) for u in range(N)]
    swap = (order[0] == xo).astype(jnp.int32)
    sends = [order[0] + swap * (order[1] - order[0]), order[1] + swap * (order[0] - order[1]), order[2], order[3]]

    products(x)
    take(r_buf, rr, xl, 2)
    take(r_buf, rr, xl, 3)
    products(xl)
    take(r_buf, rr, xr, 0)
    take(r_buf, rr, xr, 1)
    products(xr)
    greeted(1, 2)
    greet(2, 4)
    relay(m_buf, ms.at[0, 4], mr, yl, 0, to_yr)
    relay(m_buf, ms.at[1, 4], mr, yr, 2, to_yl)

    def spread(u):
        ab = sends[u]
        send(q_buf.at[ab, x], q_buf.at[ab, x], qs.at[0, u], qr.at[ab, x, 0], to_xr)
        send(q_buf.at[ab, x], q_buf.at[ab, x], qs.at[1, u], qr.at[ab, x, 0], to_xl)

    def pass_on(u):
        ab = order[u]
        arrived(q_buf.at[ab, xl], qr.at[ab, xl, 0])
        part = q_buf.at[ab, xl, pl.ds(0, B // 2)]
        send(part, part, qs.at[2, u], qr.at[ab, xl, 0], to_xr)
        arrived(q_buf.at[ab, xr], qr.at[ab, xr, 0])
        part = q_buf.at[ab, xr, pl.ds(B // 2, B // 2)]
        send(part, part, qs.at[3, u], qr.at[ab, xr, 1], to_xl)

    def last_part(u):
        ab = order[u]
        arrived(q_buf.at[ab, xo, pl.ds(0, B // 2)], qr.at[ab, xo, 0])
        arrived(q_buf.at[ab, xo, pl.ds(B // 2, B // 2)], qr.at[ab, xo, 1])

    def terms(u, blocks, add):
        ab = order[u]
        for half in range(2):
            total = s_buf[u, half] if add else None
            for xk in blocks:
                cols = pl.ds(pl.multiple_of(xk * N * B, N * B), N * B)
                rhs = m_buf[2 * half : 2 * half + 2, :, cols].reshape(2 * B, N * B)
                value = dot_nt(q_buf[ab, xk], rhs)
                total = value if total is None else total + value
            s_buf[u, half] = total

    def exchange(u):
        send(s_buf.at[u, 1 - c], e_buf.at[u], es.at[u], er.at[u], twin)

    homes = []
    place = z % N
    collector = c == place // 2

    own = [ab == group for ab in order]

    def start_if(condition, copy):
        pl.when(condition)(copy.start)
        homes.append((condition, copy))

    def gather(u):
        arrived(e_buf.at[u], er.at[u])
        s_buf[u, c] = s_buf[u, c] + e_buf[u]
        for k in range(2):
            t_buf[u, k] = s_buf[u, c, :, k * B : (k + 1) * B].astype(BF16)
            there = 2 * c + k
            away = pltpu.make_async_remote_copy(
                src_ref=t_buf.at[u, k], dst_ref=l1_buf.at[u, place], send_sem=l1s.at[u, k], recv_sem=l1r.at[u, place],
                device_id=((group * N + there) * 2 + c, row), device_id_type=MESH,
            )
            start_if(jnp.logical_not(own[u]) & (there != place), away)
        for k in range(2):
            for c2 in range(2):
                src = t_buf.at[u, k, pl.ds(c2 * B // 2, B // 2)]
                z2, y2, dst = group * N + y, 2 * c + k, g_buf.at[3 + place]
                mine = (z2 == z) & (c == c2) & (y == y2)
                local = pltpu.make_async_copy(src, dst, zr)
                away = pltpu.make_async_remote_copy(
                    src_ref=src, dst_ref=dst, send_sem=zs.at[u, 2 * c2 + k], recv_sem=zr,
                    device_id=(z2 * 2 + c2, x * N + y2), device_id_type=MESH,
                )
                pl.when(own[u] & mine)(local.start)
                start_if(own[u] & jnp.logical_not(mine), away)

    def from_group(u):
        return collector & jnp.logical_not(own[u])

    def collect(u):
        @pl.when(from_group(u))
        def _():
            total = s_buf[u, c, :, pl.ds(pl.multiple_of((place % 2) * B, B), B)]
            for k in range(1, N):
                source = (place + k) % N
                arrived(l1_buf.at[u, source], l1r.at[u, source])
                total = total + l1_buf[u, source].astype(F32)
            f_buf[u] = total.astype(BF16)
            slot = (group - order[u] + N) % N - 1
            for c2 in range(2):
                pltpu.make_async_remote_copy(
                    src_ref=f_buf.at[u, pl.ds(c2 * B // 2, B // 2)], dst_ref=g_buf.at[slot],
                    send_sem=fz.at[u, c2], recv_sem=zr,
                    device_id=((order[u] * N + y) * 2 + c2, x * N + place), device_id_type=MESH,
                ).start()

    def collected(u):
        @pl.when(from_group(u))
        def _():
            for c2 in range(2):
                pltpu.make_async_remote_copy(
                    src_ref=f_buf.at[u, pl.ds(c2 * B // 2, B // 2)], dst_ref=g_buf.at[0],
                    send_sem=fz.at[u, c2], recv_sem=zr, device_id=twin, device_id_type=MESH,
                ).wait_send()

    spread(0)
    relay(m_buf, ms.at[0, 5], mr, yl, 1, to_yr)
    relay(m_buf, ms.at[1, 5], mr, yr, 3, to_yl)
    for k in (0, 2, 1, 3):
        take(r_buf, rr, xo, k)
    products(xo)
    spread(1)
    greeted(2, 4)
    greet(3, 8)
    for block, ks in ((yl, (2, 3)), (yr, (0, 1))):
        for k in ks:
            take(m_buf, mr, block, k)
    pass_on(0)
    spread(2)
    pass_on(1)
    spread(3)
    for k in (0, 2, 1, 3):
        take(m_buf, mr, yo, k)
    last_part(0)
    terms(0, (0, 1, 2, 3), False)
    exchange(0)
    pass_on(2)
    greeted(3, 8)
    gather(0)
    last_part(1)
    terms(1, (0, 1, 2, 3), False)
    exchange(1)
    gather(1)
    pass_on(3)
    collect(0)
    last_part(2)
    terms(2, (0, 1, 2, 3), False)
    exchange(2)
    terms(3, (x, xl, xr), False)
    gather(2)
    last_part(3)
    terms(3, (xo,), True)
    exchange(3)
    collect(1)
    gather(3)
    collect(2)
    collect(3)

    pltpu.make_async_copy(g_buf, g_buf, zr).wait()
    total = g_buf[0].astype(F32)
    for k in range(1, G):
        total = total + g_buf[k].astype(F32)
    out[...] = total.astype(BF16)

    for copy in sent:
        copy.wait_send()
    for started, away in homes:
        pl.when(started)(away.wait_send)
    for u in range(N):
        collected(u)


def shards(psi, left, right, mask):
    dma = pltpu.SemaphoreType.DMA
    anywhere = pl.BlockSpec(memory_space=pl.ANY)
    return pl.pallas_call(
        kernel,
        out_shape=jax.ShapeDtypeStruct((B // 2, B), BF16),
        in_specs=[anywhere, anywhere, anywhere, pl.BlockSpec(memory_space=pltpu.SMEM)],
        out_specs=pl.BlockSpec(memory_space=pltpu.VMEM),
        scratch_shapes=[
            pltpu.VMEM((N, B, W), BF16),
            pltpu.VMEM((N, B, W), BF16),
            pltpu.VMEM((N, B, W), BF16),
            pltpu.VMEM((B, W), BF16),
            pltpu.VMEM((N, N, B, N * B), BF16),
            pltpu.VMEM((N, 2, B, 2 * B), F32),
            pltpu.VMEM((N, B, 2 * B), F32),
            pltpu.VMEM((N, 2, B, B), BF16),
            pltpu.VMEM((G, B // 2, B), BF16),
            pltpu.VMEM((N, N, B, B), BF16),
            pltpu.VMEM((N, B, B), BF16),
            dma((3,)),
            dma((2, 6)), dma((N, 4)),
            dma((2, 3)), dma((N, 4)), dma((6,)),
            dma((2, 6)), dma((N, 4)),
            dma((4, N)), dma((N, N, 2)),
            dma((N,)), dma((N,)),
            dma((N, 4)), dma, dma((N, 2)), dma((N, 2)), dma((N, N)),
            pltpu.SemaphoreType.REGULAR((4, 2)), pltpu.SemaphoreType.REGULAR((3,)),
        ],
        compiler_params=pltpu.CompilerParams(
            collective_id=0, has_side_effects=True, vmem_limit_bytes=60 << 20
        ),
    )(psi, left, right, mask).T


def solution(mesh):
    in_specs = (P("row", None), P("term", "row", None), P("term", "row", None), P("term", "row", None))
    return jax.shard_map(
        shards, mesh=mesh, in_specs=in_specs, out_specs=P("row", "term"), check_vma=False
    )
```

```python
import jax
import jax.numpy as jnp
from jax import lax
from jax.experimental import pallas as pl
from jax.experimental.pallas import tpu as pltpu
from jax.sharding import PartitionSpec as P

MESH = pl.DeviceIdType.MESH
N = 4
NZ = 16
G = N - 1 + N
B = 128
CH = 32
W = 2048
ORDER = ((0, 1, 2, 3), (0, 3, 2, 1), (0, 1, 3, 2), (0, 1, 2, 3))
F32 = jnp.float32
BF16 = jnp.bfloat16


def dot_nt(a, b):
    return lax.dot_general(a, b, (((1,), (1,)), ((), ())), preferred_element_type=F32)


def kernel(
    psi, left, right, mask, out,
    p_buf, r_buf, m_buf, l_buf, q_buf, s_buf, e_buf, t_buf, g_buf, l1_buf, f_buf,
    load_sem, rs, rr, ps, pr, fs, ms, mr, qs, qr, es, er, zs, zr, fz, l1s, l1r, hs, gs,
):
    t = lax.axis_index("term")
    row = lax.axis_index("row")
    z, c = t // 2, t % 2
    x, y = row // N, row % N
    xl, xr, xo = (x + 3) % N, (x + 1) % N, (x + 2) % N
    yl, yr, yo = (y + 3) % N, (y + 1) % N, (y + 2) % N
    to_xl, to_xr = (t, xl * N + y), (t, xr * N + y)
    to_yl, to_yr = (t, x * N + yl), (t, x * N + yr)
    twin = (z * 2 + 1 - c, row)

    def along_z(step):
        return (((z + step + NZ) % NZ) * 2 + c, row)

    sent = []

    def send(src, dst, ssem, rsem, device):
        copy = pltpu.make_async_remote_copy(
            src_ref=src, dst_ref=dst, send_sem=ssem, recv_sem=rsem, device_id=device, device_id_type=MESH
        )
        copy.start()
        sent.append(copy)

    def arrived(dst, rsem):
        pltpu.make_async_remote_copy(
            src_ref=dst, dst_ref=dst, send_sem=rsem, recv_sem=rsem, device_id=twin, device_id_type=MESH
        ).wait_recv()

    load_r = pltpu.make_async_copy(right.at[0], r_buf.at[x], load_sem.at[0])
    load_p = pltpu.make_async_copy(psi, p_buf.at[y], load_sem.at[1])
    load_l = pltpu.make_async_copy(left.at[0], l_buf, load_sem.at[2])
    barrier = pltpu.get_barrier_semaphore()
    peers = [to_xl, to_xr, to_yl, to_yr, twin, along_z(1), along_z(-1)]
    for peer in peers:
        pl.semaphore_signal(barrier, inc=1, device_id=peer, device_id_type=MESH)

    load_l.start()
    load_p.start()
    load_r.start()
    pl.semaphore_wait(barrier, len(peers))

    def greet(k, distance):
        pl.semaphore_signal(hs.at[k, 0], inc=1, device_id=along_z(distance), device_id_type=MESH)
        if 2 * distance < NZ:
            pl.semaphore_signal(hs.at[k, 1], inc=1, device_id=along_z(-distance), device_id_type=MESH)

    def greeted(k, distance):
        pl.semaphore_wait(hs.at[k, 0], 1)
        if 2 * distance < NZ:
            pl.semaphore_wait(hs.at[k, 1], 1)

    def rows(k):
        return pl.ds(k * CH, CH)

    lo = 2 * c
    for step in range(4):
        ahead, back = step, (step + 2) % 4
        if step < 2:
            send(psi.at[rows(lo + step)], p_buf.at[y, rows(lo + step)], ps.at[0, step], pr.at[y, lo + step], to_yr)
            other = lo + 1 - step
            send(psi.at[rows(other)], p_buf.at[y, rows(other)], ps.at[1, step], pr.at[y, other], to_yl)
        send(right.at[0, rows(ahead)], r_buf.at[x, rows(ahead)], rs.at[0, step], rr.at[x, ahead], to_xr)
        send(right.at[0, rows(back)], r_buf.at[x, rows(back)], rs.at[1, step], rr.at[x, back], to_xl)
    for k, device in enumerate((to_yl, to_yr)):
        pl.semaphore_signal(gs.at[k], inc=1, device_id=device, device_id_type=MESH)

    def take(buf, sem, block, k):
        arrived(buf.at[block, rows(k)], sem.at[block, k])

    def relay(buf, ssem, sem, block, k, device):
        take(buf, sem, block, k)
        send(buf.at[block, rows(k)], buf.at[block, rows(k)], ssem, sem.at[block, k], device)

    def share(block, k, n):
        send(p_buf.at[block, rows(k)], p_buf.at[block, rows(k)], fs.at[n], pr.at[block, k], twin)

    load_l.wait()
    for k in range(W // B):
        scale = jnp.full((B, B), mask[0, 0, k].astype(F32), F32).astype(BF16)
        m_buf[y, :, k * B : (k + 1) * B] = l_buf[:, k * B : (k + 1) * B] * scale

    relay(p_buf, ps.at[0, 2], pr, yl, lo, to_yr)
    relay(p_buf, ps.at[1, 2], pr, yr, lo + 1, to_yl)
    for step in range(4):
        ahead, back = step, (step + 2) % 4
        send(m_buf.at[y, rows(ahead)], m_buf.at[y, rows(ahead)], ms.at[0, step], mr.at[y, ahead], to_yr)
        send(m_buf.at[y, rows(back)], m_buf.at[y, rows(back)], ms.at[1, step], mr.at[y, back], to_yl)
    share(yl, lo, 0)
    share(yr, lo + 1, 1)
    relay(r_buf, rs.at[0, 4], rr, xl, 0, to_xr)
    relay(r_buf, rs.at[1, 4], rr, xr, 2, to_xl)
    pl.semaphore_wait(gs.at[0], 1)
    pl.semaphore_wait(gs.at[1], 1)
    pl.semaphore_signal(gs.at[2], inc=1, device_id=twin, device_id_type=MESH)
    pl.semaphore_wait(gs.at[2], 1)
    take(p_buf, pr, yl, lo + 1)
    share(yl, lo + 1, 2)
    take(p_buf, pr, yr, lo)
    share(yr, lo, 3)
    relay(r_buf, rs.at[0, 5], rr, xl, 1, to_xr)
    relay(r_buf, rs.at[1, 5], rr, xr, 3, to_xl)
    greet(0, 1)
    take(p_buf, pr, yo, lo)
    share(yo, lo, 4)
    take(p_buf, pr, yo, lo + 1)
    share(yo, lo + 1, 5)
    for block in (yl, yr, yo):
        for k in range(2):
            take(p_buf, pr, block, 2 - lo + k)
    load_p.wait()
    load_r.wait()
    greeted(0, 1)
    greet(1, 2)

    def products(block):
        for half in range(2):
            value = dot_nt(r_buf[block], p_buf[2 * half : 2 * half + 2].reshape(2 * B, W))
            q_buf[block, x, :, 2 * half * B : 2 * (half + 1) * B] = value.astype(BF16)

    group = z // N
    order = [sum((group == k).astype(jnp.int32) * ORDER[k][u] for k in range(N)) for u in range(N)]
    swap = (order[0] == xo).astype(jnp.int32)
    sends = [order[0] + swap * (order[1] - order[0]), order[1] + swap * (order[0] - order[1]), order[2], order[3]]

    products(x)
    take(r_buf, rr, xl, 2)
    take(r_buf, rr, xl, 3)
    products(xl)
    take(r_buf, rr, xr, 0)
    take(r_buf, rr, xr, 1)
    products(xr)
    greeted(1, 2)
    greet(2, 4)
    relay(m_buf, ms.at[0, 4], mr, yl, 0, to_yr)
    relay(m_buf, ms.at[1, 4], mr, yr, 2, to_yl)

    def spread(u):
        ab = sends[u]
        send(q_buf.at[ab, x], q_buf.at[ab, x], qs.at[0, u], qr.at[ab, x, 0], to_xr)
        send(q_buf.at[ab, x], q_buf.at[ab, x], qs.at[1, u], qr.at[ab, x, 0], to_xl)

    def pass_on(u):
        ab = order[u]
        arrived(q_buf.at[ab, xl], qr.at[ab, xl, 0])
        part = q_buf.at[ab, xl, pl.ds(0, B // 2)]
        send(part, part, qs.at[2, u], qr.at[ab, xl, 0], to_xr)
        arrived(q_buf.at[ab, xr], qr.at[ab, xr, 0])
        part = q_buf.at[ab, xr, pl.ds(B // 2, B // 2)]
        send(part, part, qs.at[3, u], qr.at[ab, xr, 1], to_xl)

    def last_part(u):
        ab = order[u]
        arrived(q_buf.at[ab, xo, pl.ds(0, B // 2)], qr.at[ab, xo, 0])
        arrived(q_buf.at[ab, xo, pl.ds(B // 2, B // 2)], qr.at[ab, xo, 1])

    def terms(u, blocks, add):
        ab = order[u]
        for half in range(2):
            total = s_buf[u, half] if add else None
            for xk in blocks:
                cols = pl.ds(pl.multiple_of(xk * N * B, N * B), N * B)
                rhs = m_buf[2 * half : 2 * half + 2, :, cols].reshape(2 * B, N * B)
                value = dot_nt(q_buf[ab, xk], rhs)
                total = value if total is None else total + value
            s_buf[u, half] = total

    def exchange(u):
        send(s_buf.at[u, 1 - c], e_buf.at[u], es.at[u], er.at[u], twin)

    homes = []
    place = z % N
    collector = c == place // 2

    own = [ab == group for ab in order]

    def start_if(condition, copy):
        pl.when(condition)(copy.start)
        homes.append((condition, copy))

    def gather(u):
        arrived(e_buf.at[u], er.at[u])
        s_buf[u, c] = s_buf[u, c] + e_buf[u]
        for k in range(2):
            t_buf[u, k] = s_buf[u, c, :, k * B : (k + 1) * B].astype(BF16)
            there = 2 * c + k
            away = pltpu.make_async_remote_copy(
                src_ref=t_buf.at[u, k], dst_ref=l1_buf.at[u, place], send_sem=l1s.at[u, k], recv_sem=l1r.at[u, place],
                device_id=((group * N + there) * 2 + c, row), device_id_type=MESH,
            )
            start_if(jnp.logical_not(own[u]) & (there != place), away)
        for k in range(2):
            for c2 in range(2):
                src = t_buf.at[u, k, pl.ds(c2 * B // 2, B // 2)]
                z2, y2, dst = group * N + y, 2 * c + k, g_buf.at[3 + place]
                mine = (z2 == z) & (c == c2) & (y == y2)
                local = pltpu.make_async_copy(src, dst, zr)
                away = pltpu.make_async_remote_copy(
                    src_ref=src, dst_ref=dst, send_sem=zs.at[u, 2 * c2 + k], recv_sem=zr,
                    device_id=(z2 * 2 + c2, x * N + y2), device_id_type=MESH,
                )
                pl.when(own[u] & mine)(local.start)
                start_if(own[u] & jnp.logical_not(mine), away)

    def from_group(u):
        return collector & jnp.logical_not(own[u])

    def collect(u):
        @pl.when(from_group(u))
        def _():
            total = s_buf[u, c, :, pl.ds(pl.multiple_of((place % 2) * B, B), B)]
            for k in range(1, N):
                source = (place + k) % N
                arrived(l1_buf.at[u, source], l1r.at[u, source])
                total = total + l1_buf[u, source].astype(F32)
            f_buf[u] = total.astype(BF16)
            slot = (group - order[u] + N) % N - 1
            for c2 in range(2):
                pltpu.make_async_remote_copy(
                    src_ref=f_buf.at[u, pl.ds(c2 * B // 2, B // 2)], dst_ref=g_buf.at[slot],
                    send_sem=fz.at[u, c2], recv_sem=zr,
                    device_id=((order[u] * N + y) * 2 + c2, x * N + place), device_id_type=MESH,
                ).start()

    def collected(u):
        @pl.when(from_group(u))
        def _():
            for c2 in range(2):
                pltpu.make_async_remote_copy(
                    src_ref=f_buf.at[u, pl.ds(c2 * B // 2, B // 2)], dst_ref=g_buf.at[0],
                    send_sem=fz.at[u, c2], recv_sem=zr, device_id=twin, device_id_type=MESH,
                ).wait_send()

    spread(0)
    relay(m_buf, ms.at[0, 5], mr, yl, 1, to_yr)
    relay(m_buf, ms.at[1, 5], mr, yr, 3, to_yl)
    for k in (0, 2, 1, 3):
        take(r_buf, rr, xo, k)
    products(xo)
    spread(1)
    greeted(2, 4)
    greet(3, 8)
    for block, ks in ((yl, (2, 3)), (yr, (0, 1))):
        for k in ks:
            take(m_buf, mr, block, k)
    pass_on(0)
    spread(2)
    pass_on(1)
    spread(3)
    for k in (0, 2, 1, 3):
        take(m_buf, mr, yo, k)
    last_part(0)
    terms(0, (0, 1, 2, 3), False)
    exchange(0)
    pass_on(2)
    greeted(3, 8)
    gather(0)
    last_part(1)
    terms(1, (0, 1, 2, 3), False)
    exchange(1)
    gather(1)
    pass_on(3)
    collect(0)
    last_part(2)
    terms(2, (0, 1, 2, 3), False)
    exchange(2)
    terms(3, (x, xl, xr), False)
    gather(2)
    last_part(3)
    terms(3, (xo,), True)
    exchange(3)
    collect(1)
    gather(3)
    collect(2)
    collect(3)

    pltpu.make_async_copy(g_buf, g_buf, zr).wait()
    total = g_buf[0].astype(F32)
    for k in range(1, G):
        total = total + g_buf[k].astype(F32)
    out[...] = total.astype(BF16)

    for copy in sent:
        copy.wait_send()
    for started, away in homes:
        pl.when(started)(away.wait_send)
    for u in range(N):
        collected(u)


def shards(psi, left, right, mask):
    dma = pltpu.SemaphoreType.DMA
    anywhere = pl.BlockSpec(memory_space=pl.ANY)
    return pl.pallas_call(
        kernel,
        out_shape=jax.ShapeDtypeStruct((B // 2, B), BF16),
        in_specs=[anywhere, anywhere, anywhere, pl.BlockSpec(memory_space=pltpu.SMEM)],
        out_specs=pl.BlockSpec(memory_space=pltpu.VMEM),
        scratch_shapes=[
            pltpu.VMEM((N, B, W), BF16),
            pltpu.VMEM((N, B, W), BF16),
            pltpu.VMEM((N, B, W), BF16),
            pltpu.VMEM((B, W), BF16),
            pltpu.VMEM((N, N, B, N * B), BF16),
            pltpu.VMEM((N, 2, B, 2 * B), F32),
            pltpu.VMEM((N, B, 2 * B), F32),
            pltpu.VMEM((N, 2, B, B), BF16),
            pltpu.VMEM((G, B // 2, B), BF16),
            pltpu.VMEM((N, N, B, B), BF16),
            pltpu.VMEM((N, B, B), BF16),
            dma((3,)),
            dma((2, 6)), dma((N, 4)),
            dma((2, 3)), dma((N, 4)), dma((6,)),
            dma((2, 6)), dma((N, 4)),
            dma((4, N)), dma((N, N, 2)),
            dma((N,)), dma((N,)),
            dma((N, 4)), dma, dma((N, 2)), dma((N, 2)), dma((N, N)),
            pltpu.SemaphoreType.REGULAR((4, 2)), pltpu.SemaphoreType.REGULAR((3,)),
        ],
        compiler_params=pltpu.CompilerParams(
            collective_id=0, has_side_effects=True, vmem_limit_bytes=60 << 20
        ),
    )(psi, left, right, mask).T


def solution(mesh):
    in_specs = (P("row", None), P("term", "row", None), P("term", "row", None), P("term", "row", None))
    return jax.shard_map(
        shards, mesh=mesh, in_specs=in_specs, out_specs=P("row", "term"), check_vma=False
    )
```
